128 devices in a mesh: dp: 128 (over y, x, z, core).
Axes of the slice: x: 4, y: 4, z: 4, core: 2. Of those that a mesh axis runs over, the one named last changes fastest.
Arguments:
- features: bfloat16 [128, 128, 8, 2048], P('dp'), may hold values from -12 to 14, as said below
- slot_mask: int32 [128, 128, 8], P('dp'), may hold values from 0 to 1, as said below
- owner: int32 [128], replicated, may hold values from 0 to 127, each once
Outputs:
- class_mean: float32 [128, 2048], P('dp')
- class_cov: float32 [128, 2048, 2048], P('dp')
The draws below stay inside these ranges and needn't reach their ends.
Inputs may be any that keep to these rules, and one draw needn't show every extreme that they name: `slot_mask`: every class has one device whose block of that class is full, so each class counts at least 8 images; about two thirds of slots hold images, with a fill rate that differs from class to class. The features of a class scatter around a class mean.
All inputs are finite; a program needn't handle non-finite values.
Results may differ from the reference program's by a relative error of at most 0.0003.
Values may be sent and summed in bfloat16 or wider, within the bound.
A program may use at most 64 MiB of HBM per device.

```python
import math
import jax
import jax.numpy as jnp
from jax import lax

F = 2048
CAP = 8
CLASSES = 128
N_DP = 128


def draw_features(key, part):
    first, second, third = jax.random.split(jax.random.fold_in(key, 11), 3)
    offset = jax.random.uniform(first, (1, CLASSES, 1, F), jnp.float32, 0.0, 2.0)
    spread = jnp.exp(jax.random.uniform(second, (1, 1, 1, F), jnp.float32, math.log(0.3), math.log(3.0)))
    noise = jnp.clip(jax.random.normal(third, (N_DP, CLASSES, CAP, F), jnp.float32), -4.0, 4.0)
    return (offset + spread * noise).astype(jnp.bfloat16)


def draw_slot_mask(key, part):
    first, second, third = jax.random.split(jax.random.fold_in(key, 23), 3)
    level = jax.random.randint(first, (1, CLASSES, 1), 30, 96)
    rolls = jax.random.randint(second, (N_DP, CLASSES, CAP), 0, 100)
    filled = (rolls < level).astype(jnp.int32)
    full_at = jax.random.randint(third, (CLASSES,), 0, N_DP)
    hit = (jnp.arange(N_DP)[:, None] == full_at[None, :])[:, :, None]
    return jnp.where(hit, 1, filled).astype(jnp.int32)


def setup_inputs(seed: int = 0) -> dict:
    seeds = jax.random.split(jax.random.key(seed), 4)
    return {
        "features": draw_features(jax.random.fold_in(seeds[3], 71), 0),
        "slot_mask": draw_slot_mask(jax.random.fold_in(seeds[3], 71), 0),
        "owner": jax.random.permutation(seeds[2], CLASSES).astype(jnp.int32),
    }


def one_class(args):
    rows, weights = args
    rows = rows.reshape(-1, rows.shape[-1]).astype(jnp.float32)
    weights = weights.reshape(-1).astype(jnp.float32)
    count = jnp.sum(weights)
    mean = jnp.sum(rows * weights[:, None], axis=0) / count
    centered = (rows - mean[None, :]) * weights[:, None]
    cov = lax.dot_general(centered, centered, (((0,), (0,)), ((), ())), precision=lax.Precision.HIGHEST, preferred_element_type=jnp.float32)
    return mean, cov / (count - 1.0)


def reference(features, slot_mask, owner):
    devices = jnp.arange(CLASSES, dtype=jnp.int32)
    match = (owner[None, :] == devices[:, None]).astype(jnp.int32)
    class_of = jnp.sum(match * devices[None, :], axis=1).astype(jnp.int32)

    def per_owner(cls):
        rows = lax.dynamic_index_in_dim(features, cls, 1, keepdims=False)
        weights = lax.dynamic_index_in_dim(slot_mask, cls, 1, keepdims=False)
        return one_class((rows, weights))

    class_mean, class_cov = lax.map(per_owner, class_of)
    return class_mean, class_cov
```

```python
import jax
import jax.numpy as jnp
from jax import lax
from jax.experimental import pallas as pl
from jax.experimental.pallas import tpu as pltpu
from jax.sharding import PartitionSpec as P

MESH = pl.DeviceIdType.MESH
N = 128
CAP = 8
F = 2048
GROUPS = (32, 32, 32, 16, 16)
LAST = GROUPS[-1]
STRIP = 256


def parts_of(index):
    return index // 32, (index // 8) % 4, (index // 2) % 4, index % 2


def shifted(me, shift):
    (y, x, z, c), (dy, dx, dz, dc) = parts_of(me), parts_of(shift)
    return ((y + dy) % 4) * 32 + ((x + dx) % 4) * 8 + ((z + dz) % 4) * 2 + (c + dc) % 2


def link_load(shift):
    load = [0] * 6
    for k, d in enumerate(parts_of(shift)[:3]):
        if d in (1, 2):
            load[2 * k] += 1
        if d in (3, 2):
            load[2 * k + 1] += 1
    return load


def send_order():
    rest, total, order = list(range(1, N)), [0] * 6, []

    def score(shift):
        after = [a + b for a, b in zip(total, link_load(shift))]
        mean = sum(after) / 6
        return sum((a - mean) ** 2 for a in after) - 3 * sum(link_load(shift)), (shift * 37) % N

    while rest:
        best = min(rest, key=score)
        rest.remove(best)
        order.append(best)
        total = [a + b for a, b in zip(total, link_load(best))]
    return order


ORDER = [0] + send_order()
STARTS = [sum(GROUPS[:g]) for g in range(len(GROUPS))]


def gather_kernel(class_of, mask_ref, feat_hbm, acc_ref, last_ref, sums_ref, count_ref,
                  feat, send, rows, xt, tally, tallies, feat_sem, send_sem, recv_sem, tally_send, tally_recv):
    me = lax.axis_index("dp")
    load = pltpu.make_async_copy(feat_hbm, feat, feat_sem)
    load.start()
    barrier = pltpu.get_barrier_semaphore()

    def greet(k, _):
        pl.semaphore_signal(barrier, inc=1, device_id=(lax.rem(me + k, N),), device_id_type=MESH)
        return 0

    lax.fori_loop(1, N, greet, 0)

    mask = mask_ref[...].astype(jnp.float32)
    tally[...] = jnp.sum(mask, axis=0, keepdims=True)
    lanes = lax.broadcasted_iota(jnp.int32, (CAP, N), 1)
    load.wait()

    def arrange(j, _):
        cls = class_of[j]
        weight = jnp.sum(jnp.where(lanes == cls, mask, 0.0), axis=1, keepdims=True)
        block = feat[cls].astype(jnp.float32) * weight
        send[j] = block.astype(jnp.bfloat16)
        return 0

    lax.fori_loop(0, N, arrange, 0, unroll=4)

    pl.semaphore_wait(barrier, N - 1)
    tally_copies = []
    for g, start in enumerate(STARTS):
        for k in range(max(start, 1), start + GROUPS[g]):
            to = shifted(me, ORDER[k])
            pltpu.make_async_remote_copy(
                send.at[to], rows.at[k], send_sem, recv_sem.at[g], device_id=(to,), device_id_type=MESH
            ).start()
            copy = pltpu.make_async_remote_copy(
                tally, tallies.at[pl.ds(k, 1)], tally_send, tally_recv, device_id=(to,), device_id_type=MESH
            )
            copy.start()
    rows[0] = send[me]
    tallies[pl.ds(0, 1)] = tally[...]

    for g, start in enumerate(STARTS):
        first = max(start, 1)
        size = start + GROUPS[g] - first
        pltpu.make_async_remote_copy(
            send.at[pl.ds(first, size)], rows.at[pl.ds(first, size)], send_sem, recv_sem.at[g],
            device_id=(me,), device_id_type=MESH,
        ).wait_recv()
        depth = GROUPS[g] * CAP
        x = rows[pl.ds(start, GROUPS[g])].reshape(depth, F)
        total = jnp.sum(x.astype(jnp.float32), axis=0, keepdims=True)
        if g == 0:
            sums_ref[...] = total
        else:
            sums_ref[...] += total
        if g == len(GROUPS) - 1:
            last_ref[...] = x
            continue
        xt[:, pl.ds(0, depth)] = x.T

        def strip(i, _, depth=depth, g=g, start=start):
            at = pl.ds(pl.multiple_of(i * STRIP, STRIP), STRIP)
            right = rows[pl.ds(start, GROUPS[g]), :, at].reshape(depth, STRIP)
            product = jnp.dot(xt[:, pl.ds(0, depth)], right, preferred_element_type=jnp.float32)
            if g == 0:
                acc_ref[:, at] = product
            else:
                acc_ref[:, at] += product
            return 0

        lax.fori_loop(0, F // STRIP, strip, 0)

    pltpu.make_async_remote_copy(
        send.at[pl.ds(1, N - 1)], rows.at[pl.ds(1, N - 1)], send_sem, recv_sem.at[0],
        device_id=(me,), device_id_type=MESH,
    ).wait_send()
    done = pltpu.make_async_remote_copy(
        tallies.at[pl.ds(1, N - 1)], tallies.at[pl.ds(1, N - 1)], tally_send, tally_recv,
        device_id=(me,), device_id_type=MESH,
    )
    done.wait_send()
    done.wait_recv()
    mine = jnp.where(lax.broadcasted_iota(jnp.int32, (N, N), 1) == class_of[me], tallies[...], 0.0)
    count_ref[0, 0] = jnp.sum(mine)


def finish_kernel(count_ref, acc_ref, last_ref, sums_ref, mean_ref, cov_hbm, lt, stage, sems):
    count = count_ref[0, 0]
    mean = sums_ref[...] / count
    mean_ref[...] = mean
    scale = 1.0 / (count - 1.0)
    lt[...] = last_ref[...].T
    column = (mean * jnp.ones((8, 1), jnp.float32)).T[:, :1]

    def out(i):
        return pltpu.make_async_copy(stage.at[i % 2], cov_hbm.at[0, pl.ds(i * STRIP, STRIP)], sems.at[i % 2])

    for i in range(F // STRIP):
        at = pl.ds(i * STRIP, STRIP)
        if i >= 2:
            out(i - 2).wait()
        product = jnp.dot(lt[at, :], last_ref[...], preferred_element_type=jnp.float32)
        left = lax.slice(column, (i * STRIP, 0), ((i + 1) * STRIP, 1)) * count
        stage[i % 2] = (acc_ref[at, :] + product - left * mean) * scale
        out(i).start()
    out(F // STRIP - 2).wait()
    out(F // STRIP - 1).wait()


def local(features, slot_mask, owner):
    index = jnp.arange(N, dtype=jnp.int32)
    match = (owner[None, :] == index[:, None]).astype(jnp.int32)
    class_of = jnp.sum(match * index[None, :], axis=1)
    vmem = pl.BlockSpec(memory_space=pltpu.VMEM)
    smem = pl.BlockSpec(memory_space=pltpu.SMEM)
    hbm = pl.BlockSpec(memory_space=pl.ANY)
    acc, last, sums, count = pl.pallas_call(
        gather_kernel,
        out_shape=(
            pltpu.VMEM((F, F), jnp.float32),
            pltpu.VMEM((LAST * CAP, F), jnp.bfloat16),
            pltpu.VMEM((1, F), jnp.float32),
            jax.ShapeDtypeStruct((1, 1), jnp.float32),
        ),
        in_specs=[smem, vmem, hbm],
        out_specs=(vmem, vmem, vmem, smem),
        scratch_shapes=[
            pltpu.VMEM((N, CAP, F), jnp.bfloat16),
            pltpu.VMEM((N, CAP, F), jnp.bfloat16),
            pltpu.VMEM((N, CAP, F), jnp.bfloat16),
            pltpu.VMEM((F, max(GROUPS) * CAP), jnp.bfloat16),
            pltpu.VMEM((1, N), jnp.float32),
            pltpu.VMEM((N, N), jnp.float32),
            pltpu.SemaphoreType.DMA,
            pltpu.SemaphoreType.DMA,
            pltpu.SemaphoreType.DMA((len(GROUPS),)),
            pltpu.SemaphoreType.DMA,
            pltpu.SemaphoreType.DMA,
        ],
        compiler_params=pltpu.CompilerParams(
            collective_id=0, has_side_effects=True, vmem_limit_bytes=40 * 1024 * 1024
        ),
        name="gather",
    )(class_of, slot_mask[0].T, features[0])
    mean, cov = pl.pallas_call(
        finish_kernel,
        out_shape=(jax.ShapeDtypeStruct((1, F), jnp.float32), jax.ShapeDtypeStruct((1, F, F), jnp.float32)),
        in_specs=[smem, vmem, vmem, vmem],
        out_specs=(vmem, hbm),
        scratch_shapes=[
            pltpu.VMEM((F, LAST * CAP), jnp.bfloat16),
            pltpu.VMEM((2, STRIP, F), jnp.float32),
            pltpu.SemaphoreType.DMA((2,)),
        ],
        compiler_params=pltpu.CompilerParams(vmem_limit_bytes=20 * 1024 * 1024),
        name="finish",
    )(count, *(pltpu.with_memory_space_constraint(a, pltpu.VMEM) for a in (acc, last, sums)))
    return mean, cov


def solution(mesh):
    return jax.shard_map(
        local,
        mesh=mesh,
        in_specs=(P("dp", None, None, None), P("dp", None, None), P()),
        out_specs=(P("dp", None), P("dp", None, None)),
        check_vma=False,
    )
```

```python
import jax
import jax.numpy as jnp
from jax import lax
from jax.experimental import pallas as pl
from jax.experimental.pallas import tpu as pltpu
from jax.sharding import PartitionSpec as P

MESH = pl.DeviceIdType.MESH
N = 128
CAP = 8
F = 2048
GROUPS = (32, 32, 32, 16, 8, 8)
ADDED = 3
LAST = sum(GROUPS[ADDED:]) * CAP
STRIP = 256
OUT_STRIPS = (128, 128) + (256,) * 7


def parts_of(index):
    return index // 32, (index // 8) % 4, (index // 2) % 4, index % 2


def shifted(me, shift):
    (y, x, z, c), (dy, dx, dz, dc) = parts_of(me), parts_of(shift)
    return ((y + dy) % 4) * 32 + ((x + dx) % 4) * 8 + ((z + dz) % 4) * 2 + (c + dc) % 2


def partner(me, shift):
    (y, x, z, c), (*ways, dc) = parts_of(me), parts_of(shift)
    dy, dx, dz = (ways[k] + ((4 - ways[(k + 1) % 3]) % 4 - ways[k]) * c for k in range(3))
    return ((y + dy) % 4) * 32 + ((x + dx) % 4) * 8 + ((z + dz) % 4) * 2 + (c + dc) % 2


def link_load(shift):
    load = [0] * 6
    for k, d in enumerate(parts_of(shift)[:3]):
        if d in (1, 2):
            load[2 * k] += 1
        if d in (3, 2):
            load[2 * k + 1] += 1
    return load


def hops(shift):
    return sum(link_load(shift))


def send_order(round_of):
    rest, total, order = list(range(1, N)), [0] * 6, []

    def score(shift):
        after = [a + b for a, b in zip(total, link_load(shift))]
        mean = sum(after) / 6
        return round_of(shift), sum((a - mean) ** 2 for a in after), (shift * 37) % N

    while rest:
        best = min(rest, key=score)
        rest.remove(best)
        order.append(best)
        total = [a + b for a, b in zip(total, link_load(best))]
    return order


RADIUS = 1
ROUNDS = 6


def round_of(shift):
    return max(hops(shift), 1) if hops(shift) <= 2 else ROUNDS


ORDER = [0] + send_order(round_of)
STARTS = [sum(GROUPS[:g]) for g in range(len(GROUPS))]
NEAR = sorted((shift for shift in range(1, N) if hops(shift) <= RADIUS), key=lambda shift: -hops(shift))


def gather_kernel(owner_hbm, mask_hbm, feat_hbm, acc_ref, last_ref, turned_ref, sums_ref, count_ref,
                  owner, mask_in, class_row, class_of, feat, send, rows, xt, tally, tallies,
                  in_sems, send_sem, recv_sem, tally_send, tally_recv, round_sems):
    me = lax.axis_index("dp")
    fetches = [
        pltpu.make_async_copy(src, dst, in_sems.at[i])
        for i, (src, dst) in enumerate(((owner_hbm, owner), (mask_hbm, mask_in), (feat_hbm, feat)))
    ]
    for fetch in fetches:
        fetch.start()
    barrier = pltpu.get_barrier_semaphore()
    for shift in NEAR:
        pl.semaphore_signal(barrier, inc=1, device_id=(shifted(me, shift),), device_id_type=MESH)

    fetches[0].wait()
    square = (N, N)
    owner_of_row = jnp.broadcast_to(owner[...], square).T
    matches = owner_of_row == lax.broadcasted_iota(jnp.int32, square, 1)
    class_row[...] = jnp.max(
        jnp.where(matches, lax.broadcasted_iota(jnp.int32, square, 0), 0), axis=0, keepdims=True
    )
    to_scalars = pltpu.make_async_copy(class_row, class_of, in_sems.at[3])
    to_scalars.start()
    fetches[1].wait()
    mask = mask_in[...].astype(jnp.float32)
    tally[...] = jnp.sum(mask, axis=0, keepdims=True)
    lanes = lax.broadcasted_iota(jnp.int32, (CAP, N), 1)
    to_scalars.wait()

    def finish_round(r):
        pl.semaphore_wait(barrier if r == 1 else round_sems.at[r - 2], len(NEAR))
        if r < ROUNDS:
            for shift in NEAR:
                pl.semaphore_signal(
                    round_sems.at[r - 1], inc=1, device_id=(shifted(me, shift),), device_id_type=MESH
                )

    finish_round(1)
    fetches[2].wait()

    def masked(j):
        cls = class_of[0, j]
        weight = jnp.sum(jnp.where(lanes == cls, mask, 0.0), axis=1, keepdims=True)
        return (feat[cls].astype(jnp.float32) * weight).astype(jnp.bfloat16)

    for r in range(1, ROUNDS + 1):
        slots = [k for k in range(1, N) if round_of(ORDER[k]) == r]
        for k in slots:
            to = partner(me, ORDER[k])
            send[to] = masked(to)
        if r > 1:
            finish_round(r)
        for k in slots:
            to = partner(me, ORDER[k])
            g = max(g for g, start in enumerate(STARTS) if start <= k)
            pltpu.make_async_remote_copy(
                send.at[to], rows.at[k], send_sem, recv_sem.at[g], device_id=(to,), device_id_type=MESH
            ).start()
            pltpu.make_async_remote_copy(
                tally, tallies.at[pl.ds(k, 1)], tally_send, tally_recv, device_id=(to,), device_id_type=MESH
            ).start()
    rows[0] = masked(me)
    tallies[pl.ds(0, 1)] = tally[...]

    for g, start in enumerate(STARTS):
        first = max(start, 1)
        size = start + GROUPS[g] - first
        pltpu.make_async_remote_copy(
            send.at[pl.ds(first, size)], rows.at[pl.ds(first, size)], send_sem, recv_sem.at[g],
            device_id=(me,), device_id_type=MESH,
        ).wait_recv()
        depth = GROUPS[g] * CAP
        x = rows[pl.ds(start, GROUPS[g])].reshape(depth, F)
        total = jnp.sum(x.astype(jnp.float32), axis=0, keepdims=True)
        if g == 0:
            sums_ref[...] = total
        else:
            sums_ref[...] += total
        if g >= ADDED:
            at = pl.ds((start - STARTS[ADDED]) * CAP, depth)
            last_ref[at] = x
            turned_ref[:, at] = x.T
            continue
        xt[:, pl.ds(0, depth)] = x.T

        def strip(i, _, depth=depth, g=g, start=start):
            at = pl.ds(pl.multiple_of(i * STRIP, STRIP), STRIP)
            right = rows[pl.ds(start, GROUPS[g]), :, at].reshape(depth, STRIP)
            product = jnp.dot(xt[:, pl.ds(0, depth)], right, preferred_element_type=jnp.float32)
            if g == 0:
                acc_ref[:, at] = product
            else:
                acc_ref[:, at] += product
            return 0

        lax.fori_loop(0, F // STRIP, strip, 0)

    pltpu.make_async_remote_copy(
        send.at[pl.ds(1, N - 1)], rows.at[pl.ds(1, N - 1)], send_sem, recv_sem.at[0],
        device_id=(me,), device_id_type=MESH,
    ).wait_send()
    done = pltpu.make_async_remote_copy(
        tallies.at[pl.ds(1, N - 1)], tallies.at[pl.ds(1, N - 1)], tally_send, tally_recv,
        device_id=(me,), device_id_type=MESH,
    )
    done.wait_send()
    done.wait_recv()
    mine = jnp.where(lax.broadcasted_iota(jnp.int32, square, 1) == class_of[0, me], tallies[...], 0.0)
    count_ref[...] = jnp.broadcast_to(jnp.sum(jnp.sum(mine, axis=0, keepdims=True), axis=1, keepdims=True), (1, N))


def finish_kernel(acc_ref, last_ref, turned_ref, sums_ref, count_ref, mean_hbm, cov_hbm, mean_ref, stage, sems):
    count = count_ref[:, :1]
    sums = sums_ref[...]
    mean = sums / count
    mean_ref[...] = mean
    copies = [pltpu.make_async_copy(mean_ref, mean_hbm, sems.at[len(OUT_STRIPS)])]
    copies[0].start()
    scale = 1.0 / (count - 1.0)
    start = 0
    for i, size in enumerate(OUT_STRIPS):
        at = pl.ds(start, size)
        product = jnp.dot(turned_ref[at, :], last_ref[...], preferred_element_type=jnp.float32)
        left = jnp.broadcast_to(sums_ref[:, at], (8, size)).T[:, :1]
        stage[at, :] = (acc_ref[at, :] + product - left * mean) * scale
        copies.append(pltpu.make_async_copy(stage.at[at], cov_hbm.at[0, at], sems.at[i]))
        copies[-1].start()
        start += size
    for copy in copies:
        copy.wait()


def local(features, slot_mask, owner):
    vmem = pl.BlockSpec(memory_space=pltpu.VMEM)
    hbm = pl.BlockSpec(memory_space=pl.ANY)
    partial_sums = pl.pallas_call(
        gather_kernel,
        out_shape=(
            pltpu.VMEM((F, F), jnp.float32),
            pltpu.VMEM((LAST, F), jnp.bfloat16),
            pltpu.VMEM((F, LAST), jnp.bfloat16),
            pltpu.VMEM((1, F), jnp.float32),
            pltpu.VMEM((1, N), jnp.float32),
        ),
        in_specs=[pl.BlockSpec(memory_space=pltpu.HBM)] * 3,
        out_specs=(vmem,) * 5,
        scratch_shapes=[
            pltpu.VMEM((1, N), jnp.int32),
            pltpu.VMEM((CAP, N), jnp.int32),
            pltpu.VMEM((1, N), jnp.int32),
            pltpu.SMEM((1, N), jnp.int32),
            pltpu.VMEM((N, CAP, F), jnp.bfloat16),
            pltpu.VMEM((N, CAP, F), jnp.bfloat16),
            pltpu.VMEM((N, CAP, F), jnp.bfloat16),
            pltpu.VMEM((F, max(GROUPS) * CAP), jnp.bfloat16),
            pltpu.VMEM((1, N), jnp.float32),
            pltpu.VMEM((N, N), jnp.float32),
            pltpu.SemaphoreType.DMA((4,)),
            pltpu.SemaphoreType.DMA,
            pltpu.SemaphoreType.DMA((len(GROUPS),)),
            pltpu.SemaphoreType.DMA,
            pltpu.SemaphoreType.DMA,
            pltpu.SemaphoreType.REGULAR((ROUNDS - 1,)),
        ],
        compiler_params=pltpu.CompilerParams(
            collective_id=0, has_side_effects=True, vmem_limit_bytes=24 * 1024 * 1024
        ),
        name="gather",
    )(*(pltpu.with_memory_space_constraint(a, pltpu.HBM) for a in (owner[None, :], slot_mask[0].T, features[0])))
    mean, cov = pl.pallas_call(
        finish_kernel,
        out_shape=(jax.ShapeDtypeStruct((1, F), jnp.float32), jax.ShapeDtypeStruct((1, F, F), jnp.float32)),
        in_specs=[vmem] * 5,
        out_specs=(hbm, hbm),
        scratch_shapes=[
            pltpu.VMEM((1, F), jnp.float32),
            pltpu.VMEM((F, F), jnp.float32),
            pltpu.SemaphoreType.DMA((len(OUT_STRIPS) + 1,)),
        ],
        compiler_params=pltpu.CompilerParams(vmem_limit_bytes=28 * 1024 * 1024),
        name="finish",
    )(*(pltpu.with_memory_space_constraint(a, pltpu.VMEM) for a in partial_sums))
    return mean, cov


def solution(mesh):
    return jax.shard_map(
        local,
        mesh=mesh,
        in_specs=(P("dp", None, None, None), P("dp", None, None), P()),
        out_specs=(P("dp", None), P("dp", None, None)),
        check_vma=False,
    )
```

```python
import jax
import jax.numpy as jnp
from jax import lax
from jax.experimental import pallas as pl
from jax.experimental.pallas import tpu as pltpu
from jax.sharding import PartitionSpec as P

MESH = pl.DeviceIdType.MESH
N = 128
CAP = 8
F = 2048
GROUPS = (32, 32, 32, 16, 8, 8)
ADDED = 3
LAST = sum(GROUPS[ADDED:]) * CAP
STRIP = 256
OUT_STRIPS = (128, 128) + (256,) * 7


def parts_of(index):
    return index // 32, (index // 8) % 4, (index // 2) % 4, index % 2


def shifted(me, shift):
    (y, x, z, c), (dy, dx, dz, dc) = parts_of(me), parts_of(shift)
    return ((y + dy) % 4) * 32 + ((x + dx) % 4) * 8 + ((z + dz) % 4) * 2 + (c + dc) % 2


def partner(me, shift):
    (y, x, z, c), (*ways, dc) = parts_of(me), parts_of(shift)
    dy, dx, dz = (way + ((4 - way) % 4 - way) * c for way in ways)
    return ((y + dy) % 4) * 32 + ((x + dx) % 4) * 8 + ((z + dz) % 4) * 2 + (c + dc) % 2


def link_load(shift):
    load = [0] * 6
    for k, d in enumerate(parts_of(shift)[:3]):
        if d in (1, 2):
            load[2 * k] += 1
        if d in (3, 2):
            load[2 * k + 1] += 1
    return load


def hops(shift):
    return sum(link_load(shift))


def send_order(round_of):
    rest, total, order = list(range(1, N)), [0] * 6, []

    def score(shift):
        after = [a + b for a, b in zip(total, link_load(shift))]
        mean = sum(after) / 6
        return round_of(shift) + (0, 0, 0, 1, 0.5, 0, 0)[hops(shift)], sum((a - mean) ** 2 for a in after), (shift * 37) % N

    while rest:
        best = min(rest, key=score)
        rest.remove(best)
        order.append(best)
        total = [a + b for a, b in zip(total, link_load(best))]
    return order


ROUNDS = 6


def round_of(shift):
    return max(hops(shift), 1) if hops(shift) <= 2 else ROUNDS


ORDER = [0] + send_order(round_of)
STARTS = [sum(GROUPS[:g]) for g in range(len(GROUPS))]
NEAR = [shift for shift in range(1, N) if hops(shift) <= 1]
OTHER_CORE = 1
TALLIED = [shift for shift in ORDER if shift % 2 == 0]


def gather_kernel(owner_hbm, mask_hbm, feat_hbm, acc_ref, last_ref, turned_ref, sums_ref, count_ref,
                  owner, mask_in, class_row, class_of, feat, send, rows, xt, tally, other_tally, chip_tally, tallies,
                  in_sems, send_sem, recv_sem, tally_send, tally_recv, round_sems):
    me = lax.axis_index("dp")
    fetches = [
        pltpu.make_async_copy(src, dst, in_sems.at[i])
        for i, (src, dst) in enumerate(((owner_hbm, owner), (mask_hbm, mask_in), (feat_hbm, feat)))
    ]
    for fetch in fetches:
        fetch.start()
    barrier = pltpu.get_barrier_semaphore()
    for shift in NEAR:
        pl.semaphore_signal(barrier, inc=1, device_id=(shifted(me, shift),), device_id_type=MESH)

    fetches[0].wait()
    square = (N, N)
    owner_of_row = jnp.broadcast_to(owner[...], square).T
    matches = owner_of_row == lax.broadcasted_iota(jnp.int32, square, 1)
    class_row[...] = jnp.max(
        jnp.where(matches, lax.broadcasted_iota(jnp.int32, square, 0), 0), axis=0, keepdims=True
    )
    to_scalars = pltpu.make_async_copy(class_row, class_of, in_sems.at[3])
    to_scalars.start()
    fetches[1].wait()
    mask = mask_in[...].astype(jnp.float32)
    tally[...] = jnp.sum(mask, axis=0, keepdims=True)
    lanes = lax.broadcasted_iota(jnp.int32, (CAP, N), 1)
    to_scalars.wait()

    def finish_round(r):
        pl.semaphore_wait(barrier if r == 1 else round_sems.at[r - 2], len(NEAR))
        if r < ROUNDS:
            for shift in NEAR:
                pl.semaphore_signal(
                    round_sems.at[r - 1], inc=1, device_id=(shifted(me, shift),), device_id_type=MESH
                )

    finish_round(1)
    fetches[2].wait()

    def masked(j):
        cls = class_of[0, j]
        weight = jnp.sum(jnp.where(lanes == cls, mask, 0.0), axis=1, keepdims=True)
        return (feat[cls].astype(jnp.float32) * weight).astype(jnp.bfloat16)

    def send_tally(k):
        pltpu.make_async_remote_copy(
            chip_tally, tallies.at[pl.ds(TALLIED.index(ORDER[k]), 1)], tally_send.at[1], tally_recv.at[1],
            device_id=(partner(me, ORDER[k]),), device_id_type=MESH,
        ).start()

    for r in range(1, ROUNDS + 1):
        slots = [k for k in range(1, N) if round_of(ORDER[k]) == r]
        for k in slots:
            to = partner(me, ORDER[k])
            send[to] = masked(to)
        if r > 1:
            finish_round(r)
        if r == 2:
            other = pltpu.make_async_remote_copy(
                tally, other_tally, tally_send.at[0], tally_recv.at[0], device_id=(me,), device_id_type=MESH
            )
            other.wait_send()
            other.wait_recv()
            chip_tally[...] = tally[...] + other_tally[...]
            for k in range(1, slots[0]):
                if ORDER[k] % 2 == 0:
                    send_tally(k)
        for k in slots:
            to = partner(me, ORDER[k])
            g = max(g for g, start in enumerate(STARTS) if start <= k)
            pltpu.make_async_remote_copy(
                send.at[to], rows.at[k], send_sem, recv_sem.at[g], device_id=(to,), device_id_type=MESH
            ).start()
            if ORDER[k] == OTHER_CORE:
                pltpu.make_async_remote_copy(
                    tally, other_tally, tally_send.at[0], tally_recv.at[0], device_id=(to,), device_id_type=MESH
                ).start()
            elif ORDER[k] % 2 == 0 and r > 1:
                send_tally(k)
    rows[0] = masked(me)
    tallies[pl.ds(0, 1)] = chip_tally[...]

    for g, start in enumerate(STARTS):
        first = max(start, 1)
        size = start + GROUPS[g] - first
        pltpu.make_async_remote_copy(
            send.at[pl.ds(first, size)], rows.at[pl.ds(first, size)], send_sem, recv_sem.at[g],
            device_id=(me,), device_id_type=MESH,
        ).wait_recv()
        depth = GROUPS[g] * CAP
        x = rows[pl.ds(start, GROUPS[g])].reshape(depth, F)
        total = jnp.sum(x.astype(jnp.float32), axis=0, keepdims=True)
        if g == 0:
            sums_ref[...] = total
        else:
            sums_ref[...] += total
        if g >= ADDED:
            at = pl.ds((start - STARTS[ADDED]) * CAP, depth)
            last_ref[at] = x
            turned_ref[:, at] = x.T
            continue
        xt[:, pl.ds(0, depth)] = x.T

        def strip(i, _, depth=depth, g=g, start=start):
            at = pl.ds(pl.multiple_of(i * STRIP, STRIP), STRIP)
            right = rows[pl.ds(start, GROUPS[g]), :, at].reshape(depth, STRIP)
            product = jnp.dot(xt[:, pl.ds(0, depth)], right, preferred_element_type=jnp.float32)
            if g == 0:
                acc_ref[:, at] = product
            else:
                acc_ref[:, at] += product
            return 0

        lax.fori_loop(0, F // STRIP, strip, 0)

    pltpu.make_async_remote_copy(
        send.at[pl.ds(1, N - 1)], rows.at[pl.ds(1, N - 1)], send_sem, recv_sem.at[0],
        device_id=(me,), device_id_type=MESH,
    ).wait_send()
    others = tallies.at[pl.ds(1, len(TALLIED) - 1)]
    done = pltpu.make_async_remote_copy(
        others, others, tally_send.at[1], tally_recv.at[1], device_id=(me,), device_id_type=MESH
    )
    done.wait_send()
    done.wait_recv()
    lanes = lax.broadcasted_iota(jnp.int32, (len(TALLIED), N), 1)
    mine = jnp.where(lanes == class_of[0, me], tallies[...], 0.0)
    count_ref[...] = jnp.broadcast_to(jnp.sum(jnp.sum(mine, axis=0, keepdims=True), axis=1, keepdims=True), (1, N))


def finish_kernel(acc_ref, last_ref, turned_ref, sums_ref, count_ref, mean_hbm, cov_hbm, mean_ref, stage, sems):
    count = count_ref[:, :1]
    sums = sums_ref[...]
    mean = sums / count
    mean_ref[...] = mean
    copies = [pltpu.make_async_copy(mean_ref, mean_hbm, sems.at[len(OUT_STRIPS)])]
    copies[0].start()
    scale = 1.0 / (count - 1.0)
    start = 0
    for i, size in enumerate(OUT_STRIPS):
        at = pl.ds(start, size)
        product = jnp.dot(turned_ref[at, :], last_ref[...], preferred_element_type=jnp.float32)
        left = jnp.broadcast_to(sums_ref[:, at], (8, size)).T[:, :1]
        stage[at, :] = (acc_ref[at, :] + product - left * mean) * scale
        copies.append(pltpu.make_async_copy(stage.at[at], cov_hbm.at[0, at], sems.at[i]))
        copies[-1].start()
        start += size
    for copy in copies:
        copy.wait()


def local(features, slot_mask, owner):
    vmem = pl.BlockSpec(memory_space=pltpu.VMEM)
    hbm = pl.BlockSpec(memory_space=pl.ANY)
    partial_sums = pl.pallas_call(
        gather_kernel,
        out_shape=(
            pltpu.VMEM((F, F), jnp.float32),
            pltpu.VMEM((LAST, F), jnp.bfloat16),
            pltpu.VMEM((F, LAST), jnp.bfloat16),
            pltpu.VMEM((1, F), jnp.float32),
            pltpu.VMEM((1, N), jnp.float32),
        ),
        in_specs=[pl.BlockSpec(memory_space=pltpu.HBM)] * 3,
        out_specs=(vmem,) * 5,
        scratch_shapes=[
            pltpu.VMEM((1, N), jnp.int32),
            pltpu.VMEM((CAP, N), jnp.int32),
            pltpu.VMEM((1, N), jnp.int32),
            pltpu.SMEM((1, N), jnp.int32),
            pltpu.VMEM((N, CAP, F), jnp.bfloat16),
            pltpu.VMEM((N, CAP, F), jnp.bfloat16),
            pltpu.VMEM((N, CAP, F), jnp.bfloat16),
            pltpu.VMEM((F, max(GROUPS) * CAP), jnp.bfloat16),
            pltpu.VMEM((1, N), jnp.float32),
            pltpu.VMEM((1, N), jnp.float32),
            pltpu.VMEM((1, N), jnp.float32),
            pltpu.VMEM((len(TALLIED), N), jnp.float32),
            pltpu.SemaphoreType.DMA((4,)),
            pltpu.SemaphoreType.DMA,
            pltpu.SemaphoreType.DMA((len(GROUPS),)),
            pltpu.SemaphoreType.DMA((2,)),
            pltpu.SemaphoreType.DMA((2,)),
            pltpu.SemaphoreType.REGULAR((ROUNDS - 1,)),
        ],
        compiler_params=pltpu.CompilerParams(
            collective_id=0, has_side_effects=True, vmem_limit_bytes=24 * 1024 * 1024
        ),
        name="gather",
    )(*(pltpu.with_memory_space_constraint(a, pltpu.HBM) for a in (owner[None, :], slot_mask[0].T, features[0])))
    mean, cov = pl.pallas_call(
        finish_kernel,
        out_shape=(jax.ShapeDtypeStruct((1, F), jnp.float32), jax.ShapeDtypeStruct((1, F, F), jnp.float32)),
        in_specs=[vmem] * 5,
        out_specs=(hbm, hbm),
        scratch_shapes=[
            pltpu.VMEM((1, F), jnp.float32),
            pltpu.VMEM((F, F), jnp.float32),
            pltpu.SemaphoreType.DMA((len(OUT_STRIPS) + 1,)),
        ],
        compiler_params=pltpu.CompilerParams(vmem_limit_bytes=28 * 1024 * 1024),
        name="finish",
    )(*(pltpu.with_memory_space_constraint(a, pltpu.VMEM) for a in partial_sums))
    return mean, cov


def solution(mesh):
    return jax.shard_map(
        local,
        mesh=mesh,
        in_specs=(P("dp", None, None, None), P("dp", None, None), P()),
        out_specs=(P("dp", None), P("dp", None, None)),
        check_vma=False,
    )
```

```python
import jax
import jax.numpy as jnp
from jax import lax
from jax.experimental import pallas as pl
from jax.experimental.pallas import tpu as pltpu
from jax.sharding import PartitionSpec as P

MESH = pl.DeviceIdType.MESH
N = 128
CAP = 8
F = 2048
GROUPS = (32, 32, 32, 16, 8, 8)
ADDED = 3
LAST = sum(GROUPS[ADDED:]) * CAP
STRIP = 256
OUT_STRIPS = (128, 128) + (256,) * 7


def parts_of(index):
    return index // 32, (index // 8) % 4, (index // 2) % 4, index % 2


def shifted(me, shift):
    (y, x, z, c), (dy, dx, dz, dc) = parts_of(me), parts_of(shift)
    return ((y + dy) % 4) * 32 + ((x + dx) % 4) * 8 + ((z + dz) % 4) * 2 + (c + dc) % 2


def partner(me, shift):
    (y, x, z, c), (*ways, dc) = parts_of(me), parts_of(shift)
    dy, dx, dz = (way + ((4 - way) % 4 - way) * c for way in ways)
    return ((y + dy) % 4) * 32 + ((x + dx) % 4) * 8 + ((z + dz) % 4) * 2 + (c + dc) % 2


def link_load(shift):
    load = [0] * 6
    for k, d in enumerate(parts_of(shift)[:3]):
        if d in (1, 2):
            load[2 * k] += 1
        if d in (3, 2):
            load[2 * k + 1] += 1
    return load


def hops(shift):
    return sum(link_load(shift))


def send_order(round_of):
    rest, total, order = list(range(1, N)), [0] * 6, []

    def score(shift):
        after = [a + b for a, b in zip(total, link_load(shift))]
        mean = sum(after) / 6
        return round_of(shift) + (0, 0, 0, 1, 0.5, 0, 0)[hops(shift)], sum((a - mean) ** 2 for a in after), (shift * 37) % N

    while rest:
        best = min(rest, key=score)
        rest.remove(best)
        order.append(best)
        total = [a + b for a, b in zip(total, link_load(best))]
    return order


ROUNDS = 6


def round_of(shift):
    return max(hops(shift), 1) if hops(shift) <= 2 or hops(shift) == 4 and shift % 2 else ROUNDS


ORDER = [0] + send_order(round_of)
STARTS = [sum(GROUPS[:g]) for g in range(len(GROUPS))]
NEAR = [shift for shift in range(1, N) if hops(shift) <= 1]
OTHER_CORE = 1
TALLIED = [shift for shift in ORDER if shift % 2 == 0]


def gather_kernel(owner_hbm, mask_hbm, feat_hbm, acc_ref, last_ref, turned_ref, sums_ref, count_ref,
                  owner, mask_in, class_row, class_of, feat, send, rows, xt, tally, other_tally, chip_tally, tallies,
                  in_sems, send_sem, recv_sem, tally_send, tally_recv, round_sems):
    me = lax.axis_index("dp")
    fetches = [
        pltpu.make_async_copy(src, dst, in_sems.at[i])
        for i, (src, dst) in enumerate(((owner_hbm, owner), (mask_hbm, mask_in), (feat_hbm, feat)))
    ]
    for fetch in fetches:
        fetch.start()
    barrier = pltpu.get_barrier_semaphore()
    for shift in NEAR:
        pl.semaphore_signal(barrier, inc=1, device_id=(shifted(me, shift),), device_id_type=MESH)

    fetches[0].wait()
    square = (N, N)
    owner_of_row = jnp.broadcast_to(owner[...], square).T
    matches = owner_of_row == lax.broadcasted_iota(jnp.int32, square, 1)
    class_row[...] = jnp.max(
        jnp.where(matches, lax.broadcasted_iota(jnp.int32, square, 0), 0), axis=0, keepdims=True
    )
    to_scalars = pltpu.make_async_copy(class_row, class_of, in_sems.at[3])
    to_scalars.start()
    fetches[1].wait()
    mask = mask_in[...].astype(jnp.float32)
    tally[...] = jnp.sum(mask, axis=0, keepdims=True)
    lanes = lax.broadcasted_iota(jnp.int32, (CAP, N), 1)
    to_scalars.wait()

    def finish_round(r):
        pl.semaphore_wait(barrier if r == 1 else round_sems.at[r - 2], len(NEAR))
        if r < ROUNDS:
            for shift in NEAR:
                pl.semaphore_signal(
                    round_sems.at[r - 1], inc=1, device_id=(shifted(me, shift),), device_id_type=MESH
                )

    finish_round(1)
    fetches[2].wait()

    def masked(j):
        cls = class_of[0, j]
        weight = jnp.sum(jnp.where(lanes == cls, mask, 0.0), axis=1, keepdims=True)
        return (feat[cls].astype(jnp.float32) * weight).astype(jnp.bfloat16)

    def send_tally(k):
        pltpu.make_async_remote_copy(
            chip_tally, tallies.at[pl.ds(TALLIED.index(ORDER[k]), 1)], tally_send.at[1], tally_recv.at[1],
            device_id=(partner(me, ORDER[k]),), device_id_type=MESH,
        ).start()

    for r in range(1, ROUNDS + 1):
        slots = [k for k in range(1, N) if round_of(ORDER[k]) == r]
        for k in slots:
            to = partner(me, ORDER[k])
            send[to] = masked(to)
        if r > 1:
            finish_round(r)
        if r == 2:
            other = pltpu.make_async_remote_copy(
                tally, other_tally, tally_send.at[0], tally_recv.at[0], device_id=(me,), device_id_type=MESH
            )
            other.wait_send()
            other.wait_recv()
            chip_tally[...] = tally[...] + other_tally[...]
            for k in range(1, slots[0]):
                if ORDER[k] % 2 == 0:
                    send_tally(k)
        for k in slots:
            to = partner(me, ORDER[k])
            g = max(g for g, start in enumerate(STARTS) if start <= k)
            pltpu.make_async_remote_copy(
                send.at[to], rows.at[k], send_sem, recv_sem.at[g], device_id=(to,), device_id_type=MESH
            ).start()
            if ORDER[k] == OTHER_CORE:
                pltpu.make_async_remote_copy(
                    tally, other_tally, tally_send.at[0], tally_recv.at[0], device_id=(to,), device_id_type=MESH
                ).start()
            elif ORDER[k] % 2 == 0 and r > 1:
                send_tally(k)
    rows[0] = masked(me)
    tallies[pl.ds(0, 1)] = chip_tally[...]

    for g, start in enumerate(STARTS):
        first = max(start, 1)
        size = start + GROUPS[g] - first
        pltpu.make_async_remote_copy(
            send.at[pl.ds(first, size)], rows.at[pl.ds(first, size)], send_sem, recv_sem.at[g],
            device_id=(me,), device_id_type=MESH,
        ).wait_recv()
        depth = GROUPS[g] * CAP
        x = rows[pl.ds(start, GROUPS[g])].reshape(depth, F)
        total = jnp.sum(x.astype(jnp.float32), axis=0, keepdims=True)
        if g == 0:
            sums_ref[...] = total
        else:
            sums_ref[...] += total
        if g >= ADDED:
            at = pl.ds((start - STARTS[ADDED]) * CAP, depth)
            last_ref[at] = x
            turned_ref[:, at] = x.T
            continue
        xt[:, pl.ds(0, depth)] = x.T

        def strip(i, _, depth=depth, g=g, start=start):
            at = pl.ds(pl.multiple_of(i * STRIP, STRIP), STRIP)
            right = rows[pl.ds(start, GROUPS[g]), :, at].reshape(depth, STRIP)
            product = jnp.dot(xt[:, pl.ds(0, depth)], right, preferred_element_type=jnp.float32)
            if g == 0:
                acc_ref[:, at] = product
            else:
                acc_ref[:, at] += product
            return 0

        lax.fori_loop(0, F // STRIP, strip, 0)

    pltpu.make_async_remote_copy(
        send.at[pl.ds(1, N - 1)], rows.at[pl.ds(1, N - 1)], send_sem, recv_sem.at[0],
        device_id=(me,), device_id_type=MESH,
    ).wait_send()
    others = tallies.at[pl.ds(1, len(TALLIED) - 1)]
    done = pltpu.make_async_remote_copy(
        others, others, tally_send.at[1], tally_recv.at[1], device_id=(me,), device_id_type=MESH
    )
    done.wait_send()
    done.wait_recv()
    lanes = lax.broadcasted_iota(jnp.int32, (len(TALLIED), N), 1)
    mine = jnp.where(lanes == class_of[0, me], tallies[...], 0.0)
    count_ref[...] = jnp.broadcast_to(jnp.sum(jnp.sum(mine, axis=0, keepdims=True), axis=1, keepdims=True), (1, N))


def finish_kernel(acc_ref, last_ref, turned_ref, sums_ref, count_ref, mean_hbm, cov_hbm, mean_ref, stage, sems):
    count = count_ref[:, :1]
    sums = sums_ref[...]
    mean = sums / count
    mean_ref[...] = mean
    copies = [pltpu.make_async_copy(mean_ref, mean_hbm, sems.at[len(OUT_STRIPS)])]
    copies[0].start()
    scale = 1.0 / (count - 1.0)
    start = 0
    for i, size in enumerate(OUT_STRIPS):
        at = pl.ds(start, size)
        product = jnp.dot(turned_ref[at, :], last_ref[...], preferred_element_type=jnp.float32)
        left = jnp.broadcast_to(sums_ref[:, at], (8, size)).T[:, :1]
        stage[at, :] = (acc_ref[at, :] + product - left * mean) * scale
        copies.append(pltpu.make_async_copy(stage.at[at], cov_hbm.at[0, at], sems.at[i]))
        copies[-1].start()
        start += size
    for copy in copies:
        copy.wait()


def local(features, slot_mask, owner):
    vmem = pl.BlockSpec(memory_space=pltpu.VMEM)
    hbm = pl.BlockSpec(memory_space=pl.ANY)
    partial_sums = pl.pallas_call(
        gather_kernel,
        out_shape=(
            pltpu.VMEM((F, F), jnp.float32),
            pltpu.VMEM((LAST, F), jnp.bfloat16),
            pltpu.VMEM((F, LAST), jnp.bfloat16),
            pltpu.VMEM((1, F), jnp.float32),
            pltpu.VMEM((1, N), jnp.float32),
        ),
        in_specs=[pl.BlockSpec(memory_space=pltpu.HBM)] * 3,
        out_specs=(vmem,) * 5,
        scratch_shapes=[
            pltpu.VMEM((1, N), jnp.int32),
            pltpu.VMEM((CAP, N), jnp.int32),
            pltpu.VMEM((1, N), jnp.int32),
            pltpu.SMEM((1, N), jnp.int32),
            pltpu.VMEM((N, CAP, F), jnp.bfloat16),
            pltpu.VMEM((N, CAP, F), jnp.bfloat16),
            pltpu.VMEM((N, CAP, F), jnp.bfloat16),
            pltpu.VMEM((F, max(GROUPS) * CAP), jnp.bfloat16),
            pltpu.VMEM((1, N), jnp.float32),
            pltpu.VMEM((1, N), jnp.float32),
            pltpu.VMEM((1, N), jnp.float32),
            pltpu.VMEM((len(TALLIED), N), jnp.float32),
            pltpu.SemaphoreType.DMA((4,)),
            pltpu.SemaphoreType.DMA,
            pltpu.SemaphoreType.DMA((len(GROUPS),)),
            pltpu.SemaphoreType.DMA((2,)),
            pltpu.SemaphoreType.DMA((2,)),
            pltpu.SemaphoreType.REGULAR((ROUNDS - 1,)),
        ],
        compiler_params=pltpu.CompilerParams(
            collective_id=0, has_side_effects=True, vmem_limit_bytes=24 * 1024 * 1024
        ),
        name="gather",
    )(*(pltpu.with_memory_space_constraint(a, pltpu.HBM) for a in (owner[None, :], slot_mask[0].T, features[0])))
    mean, cov = pl.pallas_call(
        finish_kernel,
        out_shape=(jax.ShapeDtypeStruct((1, F), jnp.float32), jax.ShapeDtypeStruct((1, F, F), jnp.float32)),
        in_specs=[vmem] * 5,
        out_specs=(hbm, hbm),
        scratch_shapes=[
            pltpu.VMEM((1, F), jnp.float32),
            pltpu.VMEM((F, F), jnp.float32),
            pltpu.SemaphoreType.DMA((len(OUT_STRIPS) + 1,)),
        ],
        compiler_params=pltpu.CompilerParams(vmem_limit_bytes=28 * 1024 * 1024),
        name="finish",
    )(*(pltpu.with_memory_space_constraint(a, pltpu.VMEM) for a in partial_sums))
    return mean, cov


def solution(mesh):
    return jax.shard_map(
        local,
        mesh=mesh,
        in_specs=(P("dp", None, None, None), P("dp", None, None), P()),
        out_specs=(P("dp", None), P("dp", None, None)),
        check_vma=False,
    )
```

```python
import jax
import jax.numpy as jnp
from jax import lax
from jax.experimental import pallas as pl
from jax.experimental.pallas import tpu as pltpu
from jax.sharding import PartitionSpec as P

MESH = pl.DeviceIdType.MESH
N = 128
CAP = 8
F = 2048
GROUPS = (32, 32, 32, 16, 8, 8)
ADDED = 3
LAST = sum(GROUPS[ADDED:]) * CAP
STRIP = 256
OUT_STRIPS = (128, 128) + (256,) * 7


def parts_of(index):
    return index // 32, (index // 8) % 4, (index // 2) % 4, index % 2


def shifted(me, shift):
    (y, x, z, c), (dy, dx, dz, dc) = parts_of(me), parts_of(shift)
    return ((y + dy) % 4) * 32 + ((x + dx) % 4) * 8 + ((z + dz) % 4) * 2 + (c + dc) % 2


def partner(me, shift):
    (y, x, z, c), (*ways, dc) = parts_of(me), parts_of(shift)
    dy, dx, dz = (way + ((4 - way) % 4 - way) * c for way in ways)
    return ((y + dy) % 4) * 32 + ((x + dx) % 4) * 8 + ((z + dz) % 4) * 2 + (c + dc) % 2


def link_load(shift):
    load = [0] * 6
    for k, d in enumerate(parts_of(shift)[:3]):
        if d in (1, 2):
            load[2 * k] += 1
        if d in (3, 2):
            load[2 * k + 1] += 1
    return load


def hops(shift):
    return sum(link_load(shift))


def send_order(round_of):
    rest, total, order = list(range(1, N)), [0] * 6, []

    def score(shift):
        after = [a + b for a, b in zip(total, link_load(shift))]
        mean = sum(after) / 6
        return round_of(shift) + (0, 0, 0, 1, 0.5, 0.2, 0)[hops(shift)], sum((a - mean) ** 2 for a in after), (shift * 37) % N

    while rest:
        best = min(rest, key=score)
        rest.remove(best)
        order.append(best)
        total = [a + b for a, b in zip(total, link_load(best))]
    return order


ROUNDS = 6


def round_of(shift):
    return max(hops(shift), 1) if hops(shift) <= 2 or hops(shift) == 4 and shift % 2 else ROUNDS


ORDER = [0] + send_order(round_of)
STARTS = [sum(GROUPS[:g]) for g in range(len(GROUPS))]
NEAR = [shift for shift in range(1, N) if hops(shift) <= 1]
OTHER_CORE = 1
TALLIED = [shift for shift in ORDER if shift % 2 == 0]


def gather_kernel(owner_hbm, mask_hbm, feat_hbm, acc_ref, last_ref, turned_ref, sums_ref, count_ref,
                  owner, mask_in, class_row, class_of, feat, send, rows, xt, tally, other_tally, chip_tally, tallies,
                  in_sems, send_sem, recv_sem, tally_send, tally_recv, round_sems):
    me = lax.axis_index("dp")
    fetches = [
        pltpu.make_async_copy(src, dst, in_sems.at[i])
        for i, (src, dst) in enumerate(((owner_hbm, owner), (mask_hbm, mask_in), (feat_hbm, feat)))
    ]
    for fetch in fetches:
        fetch.start()
    barrier = pltpu.get_barrier_semaphore()
    for shift in NEAR:
        pl.semaphore_signal(barrier, inc=1, device_id=(shifted(me, shift),), device_id_type=MESH)

    fetches[0].wait()
    square = (N, N)
    owner_of_row = jnp.broadcast_to(owner[...], square).T
    matches = owner_of_row == lax.broadcasted_iota(jnp.int32, square, 1)
    class_row[...] = jnp.max(
        jnp.where(matches, lax.broadcasted_iota(jnp.int32, square, 0), 0), axis=0, keepdims=True
    )
    to_scalars = pltpu.make_async_copy(class_row, class_of, in_sems.at[3])
    to_scalars.start()
    fetches[1].wait()
    mask = mask_in[...].astype(jnp.float32)
    tally[...] = jnp.sum(mask, axis=0, keepdims=True)
    lanes = lax.broadcasted_iota(jnp.int32, (CAP, N), 1)
    to_scalars.wait()

    def finish_round(r):
        pl.semaphore_wait(barrier if r == 1 else round_sems.at[r - 2], len(NEAR))
        if r < ROUNDS:
            for shift in NEAR:
                pl.semaphore_signal(
                    round_sems.at[r - 1], inc=1, device_id=(shifted(me, shift),), device_id_type=MESH
                )

    finish_round(1)
    fetches[2].wait()

    def masked(j):
        cls = class_of[0, j]
        weight = jnp.sum(jnp.where(lanes == cls, mask, 0.0), axis=1, keepdims=True)
        return (feat[cls].astype(jnp.float32) * weight).astype(jnp.bfloat16)

    def send_tally(k):
        pltpu.make_async_remote_copy(
            chip_tally, tallies.at[pl.ds(TALLIED.index(ORDER[k]), 1)], tally_send.at[1], tally_recv.at[1],
            device_id=(partner(me, ORDER[k]),), device_id_type=MESH,
        ).start()

    for r in range(1, ROUNDS + 1):
        slots = [k for k in range(1, N) if round_of(ORDER[k]) == r]
        for k in slots:
            to = partner(me, ORDER[k])
            send[to] = masked(to)
        if r > 1:
            finish_round(r)
        if r == 2:
            other = pltpu.make_async_remote_copy(
                tally, other_tally, tally_send.at[0], tally_recv.at[0], device_id=(me,), device_id_type=MESH
            )
            other.wait_send()
            other.wait_recv()
            chip_tally[...] = tally[...] + other_tally[...]
            for k in range(1, slots[0]):
                if ORDER[k] % 2 == 0:
                    send_tally(k)
        for k in slots:
            to = partner(me, ORDER[k])
            g = max(g for g, start in enumerate(STARTS) if start <= k)
            pltpu.make_async_remote_copy(
                send.at[to], rows.at[k], send_sem, recv_sem.at[g], device_id=(to,), device_id_type=MESH
            ).start()
            if ORDER[k] == OTHER_CORE:
                pltpu.make_async_remote_copy(
                    tally, other_tally, tally_send.at[0], tally_recv.at[0], device_id=(to,), device_id_type=MESH
                ).start()
            elif ORDER[k] % 2 == 0 and r > 1:
                send_tally(k)
    rows[0] = masked(me)
    tallies[pl.ds(0, 1)] = chip_tally[...]

    for g, start in enumerate(STARTS):
        first = max(start, 1)
        size = start + GROUPS[g] - first
        pltpu.make_async_remote_copy(
            send.at[pl.ds(first, size)], rows.at[pl.ds(first, size)], send_sem, recv_sem.at[g],
            device_id=(me,), device_id_type=MESH,
        ).wait_recv()
        depth = GROUPS[g] * CAP
        x = rows[pl.ds(start, GROUPS[g])].reshape(depth, F)
        total = jnp.sum(x.astype(jnp.float32), axis=0, keepdims=True)
        if g == 0:
            sums_ref[...] = total
        else:
            sums_ref[...] += total
        if g >= ADDED:
            at = pl.ds((start - STARTS[ADDED]) * CAP, depth)
            last_ref[at] = x
            turned_ref[:, at] = x.T
            continue
        xt[:, pl.ds(0, depth)] = x.T

        def strip(i, _, depth=depth, g=g, start=start):
            at = pl.ds(pl.multiple_of(i * STRIP, STRIP), STRIP)
            right = rows[pl.ds(start, GROUPS[g]), :, at].reshape(depth, STRIP)
            product = jnp.dot(xt[:, pl.ds(0, depth)], right, preferred_element_type=jnp.float32)
            if g == 0:
                acc_ref[:, at] = product
            else:
                acc_ref[:, at] += product
            return 0

        lax.fori_loop(0, F // STRIP, strip, 0)

    pltpu.make_async_remote_copy(
        send.at[pl.ds(1, N - 1)], rows.at[pl.ds(1, N - 1)], send_sem, recv_sem.at[0],
        device_id=(me,), device_id_type=MESH,
    ).wait_send()
    others = tallies.at[pl.ds(1, len(TALLIED) - 1)]
    done = pltpu.make_async_remote_copy(
        others, others, tally_send.at[1], tally_recv.at[1], device_id=(me,), device_id_type=MESH
    )
    done.wait_send()
    done.wait_recv()
    lanes = lax.broadcasted_iota(jnp.int32, (len(TALLIED), N), 1)
    mine = jnp.where(lanes == class_of[0, me], tallies[...], 0.0)
    count_ref[...] = jnp.broadcast_to(jnp.sum(jnp.sum(mine, axis=0, keepdims=True), axis=1, keepdims=True), (1, N))


def finish_kernel(acc_ref, last_ref, turned_ref, sums_ref, count_ref, mean_hbm, cov_hbm, mean_ref, stage, sems):
    count = count_ref[:, :1]
    sums = sums_ref[...]
    mean = sums / count
    mean_ref[...] = mean
    copies = [pltpu.make_async_copy(mean_ref, mean_hbm, sems.at[len(OUT_STRIPS)])]
    copies[0].start()
    scale = 1.0 / (count - 1.0)
    start = 0
    for i, size in enumerate(OUT_STRIPS):
        at = pl.ds(start, size)
        product = jnp.dot(turned_ref[at, :], last_ref[...], preferred_element_type=jnp.float32)
        left = jnp.broadcast_to(sums_ref[:, at], (8, size)).T[:, :1]
        stage[at, :] = (acc_ref[at, :] + product - left * mean) * scale
        copies.append(pltpu.make_async_copy(stage.at[at], cov_hbm.at[0, at], sems.at[i]))
        copies[-1].start()
        start += size
    for copy in copies:
        copy.wait()


def local(features, slot_mask, owner):
    vmem = pl.BlockSpec(memory_space=pltpu.VMEM)
    hbm = pl.BlockSpec(memory_space=pl.ANY)
    partial_sums = pl.pallas_call(
        gather_kernel,
        out_shape=(
            pltpu.VMEM((F, F), jnp.float32),
            pltpu.VMEM((LAST, F), jnp.bfloat16),
            pltpu.VMEM((F, LAST), jnp.bfloat16),
            pltpu.VMEM((1, F), jnp.float32),
            pltpu.VMEM((1, N), jnp.float32),
        ),
        in_specs=[pl.BlockSpec(memory_space=pltpu.HBM)] * 3,
        out_specs=(vmem,) * 5,
        scratch_shapes=[
            pltpu.VMEM((1, N), jnp.int32),
            pltpu.VMEM((CAP, N), jnp.int32),
            pltpu.VMEM((1, N), jnp.int32),
            pltpu.SMEM((1, N), jnp.int32),
            pltpu.VMEM((N, CAP, F), jnp.bfloat16),
            pltpu.VMEM((N, CAP, F), jnp.bfloat16),
            pltpu.VMEM((N, CAP, F), jnp.bfloat16),
            pltpu.VMEM((F, max(GROUPS) * CAP), jnp.bfloat16),
            pltpu.VMEM((1, N), jnp.float32),
            pltpu.VMEM((1, N), jnp.float32),
            pltpu.VMEM((1, N), jnp.float32),
            pltpu.VMEM((len(TALLIED), N), jnp.float32),
            pltpu.SemaphoreType.DMA((4,)),
            pltpu.SemaphoreType.DMA,
            pltpu.SemaphoreType.DMA((len(GROUPS),)),
            pltpu.SemaphoreType.DMA((2,)),
            pltpu.SemaphoreType.DMA((2,)),
            pltpu.SemaphoreType.REGULAR((ROUNDS - 1,)),
        ],
        compiler_params=pltpu.CompilerParams(
            collective_id=0, has_side_effects=True, vmem_limit_bytes=24 * 1024 * 1024
        ),
        name="gather",
    )(*(pltpu.with_memory_space_constraint(a, pltpu.HBM) for a in (owner[None, :], slot_mask[0].T, features[0])))
    mean, cov = pl.pallas_call(
        finish_kernel,
        out_shape=(jax.ShapeDtypeStruct((1, F), jnp.float32), jax.ShapeDtypeStruct((1, F, F), jnp.float32)),
        in_specs=[vmem] * 5,
        out_specs=(hbm, hbm),
        scratch_shapes=[
            pltpu.VMEM((1, F), jnp.float32),
            pltpu.VMEM((F, F), jnp.float32),
            pltpu.SemaphoreType.DMA((len(OUT_STRIPS) + 1,)),
        ],
        compiler_params=pltpu.CompilerParams(vmem_limit_bytes=28 * 1024 * 1024),
        name="finish",
    )(*(pltpu.with_memory_space_constraint(a, pltpu.VMEM) for a in partial_sums))
    return mean, cov


def solution(mesh):
    return jax.shard_map(
        local,
        mesh=mesh,
        in_specs=(P("dp", None, None, None), P("dp", None, None), P()),
        out_specs=(P("dp", None), P("dp", None, None)),
        check_vma=False,
    )
```
